32 devices in a mesh: ens: 4 (over z), gx: 2 (over x), gy: 4 (over y, core).
Axes of the slice: x: 2, y: 2, z: 4, core: 2. Of those that a mesh axis runs over, the one named last changes fastest.
Arguments:
- members: bfloat16 [64, 75, 32, 512], P(('ens', 'gx'), None, None, 'gy'), may hold values from -0.75 to 0.75
- spread: bfloat16 [75, 75], replicated, as said below
- sea_mask: int32 [32, 512], P(('ens', 'gx'), 'gy'), may hold values 0 or 1
- innovations: float32 [75, 32, 512], P(None, ('ens', 'gx'), 'gy'), may hold values from -19 to 19
- obs_error: float32 [75, 32, 512], P(None, ('ens', 'gx'), 'gy'), may hold values from 0.3 to 3
- static_scale: float32 [75, 32, 512], P(None, ('ens', 'gx'), 'gy'), may hold values from 2 to 8
Outputs:
- increment: float32 [75, 32, 512], P(None, ('ens', 'gx'), 'gy')
- alpha_fields: bfloat16 [64, 75, 32, 512], P(('ens', 'gx'), None, None, 'gy')
The draws below stay inside these ranges and needn't reach their ends.
Inputs may be any that keep to these rules, and one draw needn't show every extreme that they name: `spread`: symmetric and positive definite. `sea_mask`: 1 marks sea, 0 land.
All inputs are finite; a program needn't handle non-finite values. No bound on the sum of `sea_mask` on one device may be relied on, other than what follows from the above.
Results may differ from the reference program's by a relative error of at most 0.0065.
Values may be sent and summed in bfloat16 or wider, within the bound.
A program may use at most 128 MiB of HBM per device.

```python
import math
import jax
import jax.numpy as jnp
from jax import lax

MEMBERS = 64
LAYERS = 75
GRIDS = 3
SWEEPS = 2
COARSE_SWEEPS = 4
ITERATIONS = 3
NX = 32
NY = 512


def draw_spread(key, part):
    noise = jax.random.uniform(key, (LAYERS, LAYERS), jnp.float32, -1.0, 1.0)
    symmetric = 0.45 * (noise + noise.T) / LAYERS
    leading = 1.0 + 0.5 * jax.random.uniform(jax.random.fold_in(key, 7), (LAYERS,), jnp.float32)
    identity = jnp.eye(LAYERS, dtype=jnp.float32)
    return (symmetric * (1.0 - identity) + identity * leading[:, None]).astype(jnp.bfloat16)


def draw_innovations(key, part):
    base = jnp.clip(jax.random.normal(key, (LAYERS, NX, NY), jnp.float32), -4.0, 4.0)
    rising = 3.0 ** (jnp.arange(NX, dtype=jnp.float32) / (NX - 1))
    return 0.5 * base * rising[None, :, None]


def place_ends(drawn, own_key, least, high):
    place = [jax.random.randint(jax.random.fold_in(own_key, axis), (), 0, length) for axis, length in enumerate(drawn.shape)]
    longest = drawn.shape.index(max(drawn.shape))
    neighbour = place[:longest] + [(place[longest] + 1) % drawn.shape[longest]] + place[longest + 1:]
    return drawn.at[tuple(place)].set(least).at[tuple(neighbour)].set(high)


def steps_of(stream_key, shape, cuts, low, top_value):
    factor_of = 1.0
    for axis_at, parts in cuts:
        steps = jax.random.uniform(jax.random.fold_in(jax.random.fold_in(stream_key, 6), axis_at), (parts,), jnp.float32, low / len(cuts), top_value / len(cuts))
        factor_of = factor_of * jnp.repeat(jnp.exp(steps), shape[axis_at] // parts).reshape((-1,) + (1,) * (len(shape) - 1 - axis_at))
    return factor_of


def normal_values(key, extent, deviation, limit, split=(), kind=jnp.bfloat16):
    level = steps_of(key, extent, split, -0.22, 0.18) if split else 1.0
    result = jax.random.normal(key, extent, jnp.float32) * deviation * level
    return jnp.minimum(jnp.maximum(result, -limit), limit).astype(kind)


def setup_inputs(seed: int = 0) -> dict:
    key_list = jax.random.split(jax.random.key(seed), 7)
    return {
        "members": normal_values(key_list[0], (MEMBERS, LAYERS, NX, NY), 0.125, 0.75, ((0, 8), (3, 4))),
        "spread": draw_spread(jax.random.fold_in(key_list[6], 71), 0),
        "sea_mask": place_ends((jax.random.randint(key_list[2], (NX, NY), 0, 8) < 7).astype(jnp.int32), jax.random.fold_in(key_list[2], 1), 0, 1),
        "innovations": draw_innovations(jax.random.fold_in(key_list[6], 71), 0),
        "obs_error": jnp.clip(jnp.exp(math.log(3.0) - 2.3025851 * jax.random.uniform(key_list[4], (LAYERS, NX, NY), jnp.float32) ** steps_of(key_list[4], (LAYERS, NX, NY), ((1, 8), (2, 4)), -0.2, 0.2)), 0.3, 3.0),
        "static_scale": jnp.clip(jnp.exp(math.log(8.0) - 1.3862944 * jax.random.uniform(key_list[5], (LAYERS, NX, NY), jnp.float32) ** steps_of(key_list[5], (LAYERS, NX, NY), ((1, 8), (2, 4)), -0.2, 0.2)), 2.0, 8.0),
    }


diffusivity = 16.0
damping = 0.8


def neighbours(values):
    padded = jnp.pad(values, ((0, 0), (1, 1), (1, 1)))
    return padded[:, 2:, 1:-1] + padded[:, :-2, 1:-1] + padded[:, 1:-1, 2:] + padded[:, 1:-1, :-2]


def apply_level(values, strength):
    return values + strength * (4.0 * values - neighbours(values))


def relax(values, source, strength):
    return values + damping * (source - apply_level(values, strength)) / (1.0 + 4.0 * strength)


def restrict(values):
    layer_count, row_count, column_count = values.shape
    return 0.25 * values.reshape(layer_count, row_count // 2, 2, column_count // 2, 2).sum(axis=(2, 4))


def prolong(values):
    layer_count, row_count, column_count = values.shape
    spread_out = jnp.broadcast_to(values[:, :, None, :, None], (layer_count, row_count, 2, column_count, 2))
    return spread_out.reshape(layer_count, 2 * row_count, 2 * column_count)


def vcycle(source, grid_level):
    strength = diffusivity / 4.0 ** grid_level
    solution = damping / (1.0 + 4.0 * strength) * source
    if grid_level == GRIDS - 1:
        for sweep_index in range(COARSE_SWEEPS - 1):
            solution = relax(solution, source, strength)
        return solution
    for sweep_index in range(SWEEPS - 1):
        solution = relax(solution, source, strength)
    remainder = source - apply_level(solution, strength)
    solution = solution + prolong(vcycle(restrict(remainder), grid_level + 1))
    for sweep_index in range(SWEEPS):
        solution = relax(solution, source, strength)
    return solution


def reference(members, spread, sea_mask, innovations, obs_error, static_scale):
    sea = sea_mask.astype(jnp.float32)[None]

    def member_mix(member, masked):
        product = (member.astype(jnp.float32) * masked).astype(jnp.bfloat16)
        flat = product.reshape(LAYERS, NX * NY)
        return jnp.dot(spread, flat, preferred_element_type=jnp.float32).reshape(LAYERS, NX, NY)

    def covariance(direction):
        masked = sea * direction

        def accumulate(running, member):
            return running + member.astype(jnp.float32) * member_mix(member, masked), None

        ensemble, unused = lax.scan(accumulate, jnp.zeros((LAYERS, NX, NY), jnp.float32), members)
        static = static_scale * vcycle(static_scale * masked, 0)
        return sea * (ensemble + static)

    weights = jnp.zeros((LAYERS, NX, NY), jnp.float32)
    increment = jnp.zeros((LAYERS, NX, NY), jnp.float32)
    residual = innovations
    direction = innovations
    norm_now = jnp.sum(residual * residual)
    for iteration in range(ITERATIONS):
        cov_dir = covariance(direction)
        image = cov_dir + obs_error * direction
        alpha = norm_now / jnp.sum(direction * image)
        weights = weights + alpha * direction
        increment = increment + alpha * cov_dir
        residual = residual - alpha * image
        norm_next = jnp.sum(residual * residual)
        direction = residual + (norm_next / norm_now) * direction
        norm_now = norm_next
    final_mask = sea * weights
    alpha_fields = lax.map(lambda member: member_mix(member, final_mask).astype(jnp.bfloat16), members)
    return increment, alpha_fields
```

```python
import functools

import jax
import jax.numpy as jnp
from jax import lax
from jax.experimental import pallas as pl
from jax.experimental.pallas import tpu as pltpu
from jax.sharding import PartitionSpec as P

GRIDS = 3
SWEEPS = 2
COARSE_SWEEPS = 4
ITERATIONS = 3
SUB = 8
LANES = 128

diffusivity = 16.0
damping = 0.8
MESH = pl.DeviceIdType.MESH
F32 = jnp.float32
BF16 = jnp.bfloat16


def strength_of(level):
    return diffusivity / 4.0**level


def lane_index(width):
    return lax.broadcasted_iota(jnp.int32, (SUB, width), 1)


def over_rows(count, body):
    chunk = min(SUB, count)

    @pl.loop(0, count // chunk)
    def _(block):
        start = block * chunk
        for row in range(chunk):
            body(start + row)


def neighbours(ref, row, step):
    here = ref[row + 1]
    width = here.shape[-1]
    lane = lane_index(width)
    left = jnp.where(lane < step, 0.0, pltpu.roll(here, step, 1))
    right = jnp.where(lane >= width - step, 0.0, pltpu.roll(here, width - step, 1))
    return here, ref[row] + ref[row + 2] + left + right


def relax(src, source, dst, rows, level, scale=None):
    strength = strength_of(level)
    factor = damping / (1.0 + 4.0 * strength)

    def body(row):
        here, around = neighbours(src, row, 2**level)
        if scale is not None:
            here, around = here * scale, around * scale
        dst[row + 1] = (1.0 - damping) * here + factor * (source[row + 1] + strength * around)

    over_rows(rows, body)


def restrict_remainder(src, source, dst, rows, level):
    strength = strength_of(level)
    step = 2**level

    def one(row):
        here, around = neighbours(src, row, step)
        left_over = source[row + 1] - (1.0 + 4.0 * strength) * here + strength * around
        return left_over

    def body(row):
        both = one(2 * row) + one(2 * row + 1)
        width = both.shape[-1]
        even = lax.rem(lane_index(width) // step, 2) == 0
        other = jnp.where(even, pltpu.roll(both, width - step, 1), pltpu.roll(both, step, 1))
        dst[row + 1] = 0.25 * (both + other)

    over_rows(rows // 2, body)


def add_prolonged(dst, coarse, rows):
    def body(row):
        extra = coarse[row + 1]
        dst[2 * row + 1] = dst[2 * row + 1] + extra
        dst[2 * row + 2] = dst[2 * row + 2] + extra

    over_rows(rows // 2, body)


def vcycle(levels, level, rows):
    source, first, second = levels[level]
    factor = damping / (1.0 + 4.0 * strength_of(level))
    if level == GRIDS - 1:
        relax(source, source, first, rows, level, factor)
        for _ in range(COARSE_SWEEPS - 2):
            relax(first, source, second, rows, level)
            first, second = second, first
        return first
    relax(source, source, first, rows, level, factor)
    for _ in range(SWEEPS - 2):
        relax(first, source, second, rows, level)
        first, second = second, first
    restrict_remainder(first, source, levels[level + 1][0], rows, level)
    coarse = vcycle(levels, level + 1, rows // 2)
    add_prolonged(first, coarse, rows)
    for _ in range(SWEEPS):
        relax(first, source, second, rows, level)
        first, second = second, first
    return first


def kernel(
    sizes,
    groups,
    members,
    spread,
    sea,
    innovations,
    obs_error,
    scale,
    increment,
    alpha_fields,
    tiles,
    gathered,
    w_send,
    residual,
    direction,
    along,
    cov_dir,
    weights,
    cov_res,
    image,
    f_send,
    back,
    p_send,
    p_recv,
    f_recv,
    f_along,
    *rest,
):
    n_ens, n_gx, n_gy = sizes
    level_refs = rest[: 3 * GRIDS]
    (m_ssem, m_rsem, f_ssem, f_rsem, b_ssem, b_rsem, p_ssem, p_rsem, w_ssem, w_rsem) = rest[3 * GRIDS :]
    levels = [level_refs[3 * g : 3 * g + 3] for g in range(GRIDS)]
    f_res = levels[0][0]
    n_blocks = n_ens * n_gx
    n_dev = n_blocks * n_gy
    spacing = n_dev // groups
    block = lax.axis_index("ens") * n_gx + lax.axis_index("gx")
    column = lax.axis_index("gy")
    me = block * n_gy + column
    is_owner = (lax.rem(me, spacing) == 0) & (me // spacing < groups)
    my_group = jnp.minimum(me // spacing, groups - 1)
    tile_rows = innovations.shape[0]
    per_block = members.shape[1]
    grid_rows = tile_rows * n_blocks

    def device(rank):
        return (rank // (n_gx * n_gy), lax.rem(rank // n_gy, n_gx), lax.rem(rank, n_gy))

    def group_rows(group):
        return pl.ds(pl.multiple_of(group * SUB, SUB), SUB)

    def grid_slot(ref, rank):
        rows = pl.ds((rank // n_gy) * tile_rows + 1, tile_rows)
        lanes = pl.ds(pl.multiple_of(lax.rem(rank, n_gy) * LANES, LANES), LANES)
        return ref.at[rows, :, lanes]

    def send(src, dst, send_sem, recv_sem, rank):
        @pl.when(rank == me)
        def _():
            pltpu.make_async_copy(src, dst, recv_sem).start()

        @pl.when(rank != me)
        def _():
            pltpu.make_async_remote_copy(
                src_ref=src,
                dst_ref=dst,
                send_sem=send_sem,
                recv_sem=recv_sem,
                device_id=device(rank),
                device_id_type=MESH,
            ).start()

    def sent(src, send_sem, rank):
        @pl.when(rank != me)
        def _():
            pltpu.make_async_copy(src, src, send_sem).wait()

    def arrived(dst, recv_sem):
        pltpu.make_async_copy(dst, dst, recv_sem).wait()

    barrier = pltpu.get_barrier_semaphore()

    @pl.loop(1, n_dev)
    def _(step):
        pl.semaphore_signal(
            barrier, inc=1, device_id=device(lax.rem(me + step, n_dev)), device_id_type=MESH
        )

    for r in range(tile_rows):
        start = innovations[r]
        residual[r] = start
        f_send[r] = scale[r] * (sea[r] * start)
        zero = jnp.zeros_like(start)
        for ref in (direction, along, cov_dir, weights):
            ref[r] = zero
        increment[r] = zero

    @pl.when(is_owner)
    def _():
        for source, first, second in levels:
            for ref in (source, first, second):
                edge = jnp.zeros(ref.shape[1:], F32)
                ref[0] = edge
                ref[ref.shape[0] - 1] = edge

        def clear(row):
            f_along[row + 1] = jnp.zeros(f_along.shape[1:], F32)
            f_res[row + 1] = jnp.zeros(f_res.shape[1:], F32)

        over_rows(grid_rows, clear)

    pl.semaphore_wait(barrier, n_dev - 1)

    def send_source():
        @pl.loop(0, groups)
        def _(group):
            send(
                f_send.at[:, group_rows(group), :],
                grid_slot(f_recv, me),
                f_ssem.at[group],
                f_rsem.at[me],
                group * spacing,
            )

    def source_sent():
        @pl.loop(0, groups)
        def _(group):
            sent(f_send.at[:, group_rows(group), :], f_ssem.at[group], group * spacing)

    send_source()

    @pl.loop(0, n_blocks)
    def _(step):
        target = lax.rem(block + step, n_blocks)
        send(
            members.at[target],
            tiles.at[block],
            m_ssem.at[target],
            m_rsem.at[block],
            target * n_gy + column,
        )

    def mix(values, vector):
        product = [
            (values[r].astype(F32) * vector[r]).astype(BF16) for r in range(tile_rows)
        ]
        mixed = jnp.dot(
            spread[...], jnp.concatenate(product, axis=1), preferred_element_type=F32
        )
        return [mixed[:, r * LANES : (r + 1) * LANES] for r in range(tile_rows)]

    def iterate(iteration, carry):
        alpha, ratio, norm = carry

        @pl.when(is_owner)
        def _():
            @pl.loop(0, n_dev)
            def _(rank):
                arrived(grid_slot(f_recv, rank), f_rsem.at[rank])

            def advance(row):
                new = f_recv[row + 1] + ratio * f_along[row + 1]
                f_along[row + 1] = new
                f_res[row + 1] = f_res[row + 1] - alpha * new

            over_rows(grid_rows, advance)
            result = vcycle(levels, 0, grid_rows)

            @pl.loop(0, n_dev)
            def _(rank):
                send(
                    grid_slot(result, rank),
                    back.at[:, group_rows(my_group), :],
                    b_ssem.at[rank],
                    b_rsem.at[my_group],
                    rank,
                )

        for r in range(tile_rows):
            image[r] = sea[r] * residual[r]
            cov_res[r] = jnp.zeros_like(image[r])

        @pl.loop(0, n_blocks)
        def _(step):
            origin = lax.rem(block - step + n_blocks, n_blocks)

            @pl.when(iteration == 0)
            def _():
                arrived(tiles.at[origin], m_rsem.at[origin])

            @pl.loop(0, per_block)
            def _(k):
                values = tiles[origin, k]
                mixed = mix(values, image)
                for r in range(tile_rows):
                    cov_res[r] = cov_res[r] + values[r].astype(F32) * mixed[r]

        @pl.loop(0, groups)
        def _(group):
            arrived(back.at[:, group_rows(group), :], b_rsem.at[group])

        source_sent()
        own = jnp.zeros((1, LANES), F32)
        cross = jnp.zeros((1, LANES), F32)
        for r in range(tile_rows):
            cov = sea[r] * (cov_res[r] + scale[r] * back[r])
            now = residual[r]
            img = cov + obs_error[r] * now
            cov_res[r] = cov
            image[r] = img
            f_send[r] = scale[r] * (sea[r] * img)
            own = own + jnp.sum(now * now, axis=0, keepdims=True)
            cross = cross + jnp.sum(now * img, axis=0, keepdims=True)
        p_send[iteration, 0:1] = own
        p_send[iteration, 1:2] = cross

        @pl.loop(0, n_dev)
        def _(step):
            rank = lax.rem(me + step, n_dev)
            send(
                p_send.at[iteration],
                p_recv.at[iteration, me],
                p_ssem.at[iteration, rank],
                p_rsem.at[iteration, me],
                rank,
            )

        @pl.when(iteration < ITERATIONS - 1)
        def _():
            send_source()

        @pl.loop(0, n_dev)
        def _(rank):
            arrived(p_recv.at[iteration, rank], p_rsem.at[iteration, rank])

        total = jnp.sum(jnp.sum(p_recv[iteration], axis=0), axis=1, keepdims=True)
        norm_next, product = total[0:1], total[1:2]
        ratio = jnp.where(iteration == 0, 0.0, norm_next / norm)
        alpha = norm_next / (product - ratio * norm_next / alpha)
        for r in range(tile_rows):
            step_to = residual[r] + ratio * direction[r]
            direction[r] = step_to
            weights[r] = weights[r] + alpha * step_to
            cov = cov_res[r] + ratio * cov_dir[r]
            cov_dir[r] = cov
            increment[r] = increment[r] + alpha * cov
            img = image[r] + ratio * along[r]
            along[r] = img
            residual[r] = residual[r] - alpha * img

        @pl.loop(0, n_dev)
        def _(rank):
            sent(p_send.at[iteration], p_ssem.at[iteration, rank], rank)

        @pl.when(is_owner)
        def _():
            @pl.loop(0, n_dev)
            def _(rank):
                sent(grid_slot(levels[0][1], rank), b_ssem.at[rank], rank)

        return alpha, ratio, norm_next

    one = jnp.ones((1, 1), F32)
    lax.fori_loop(0, ITERATIONS, iterate, (-one, one * 0.0, one))

    for r in range(tile_rows):
        w_send[r] = (sea[r] * weights[r]).astype(BF16)

    @pl.loop(0, n_blocks)
    def _(step):
        target = lax.rem(block + step, n_blocks)
        send(
            w_send,
            gathered.at[block],
            w_ssem.at[target],
            w_rsem.at[block],
            target * n_gy + column,
        )

    @pl.loop(0, n_blocks)
    def _(step):
        origin = lax.rem(block - step + n_blocks, n_blocks)
        arrived(gathered.at[origin], w_rsem.at[origin])
        for r in range(tile_rows):
            image[r] = gathered[origin, r].astype(F32)

        @pl.loop(0, per_block)
        def _(k):
            mixed = mix(members[origin, k], image)
            for r in range(tile_rows):
                alpha_fields[k, origin, r] = mixed[r].astype(BF16)

    @pl.loop(0, n_blocks)
    def _(target):
        sent(w_send, w_ssem.at[target], target * n_gy + column)
        sent(members.at[target], m_ssem.at[target], target * n_gy + column)


def local(sizes, members, spread, sea_mask, innovations, obs_error, static_scale):
    n_ens, n_gx, n_gy = sizes
    n_blocks = n_ens * n_gx
    n_dev = n_blocks * n_gy
    count, layers, rows, lanes = members.shape
    tile_rows = innovations.shape[1]
    groups = -(-layers // SUB)
    padded = groups * SUB
    extra = padded - layers
    grid_rows = rows
    width = lanes * n_gy

    by_row = members.reshape(count, layers, n_blocks, tile_rows, lanes).transpose(2, 0, 3, 1, 4)
    by_row = jnp.pad(by_row, ((0, 0), (0, 0), (0, 0), (0, extra), (0, 0)))

    def field(values):
        return jnp.pad(values.transpose(1, 0, 2), ((0, 0), (0, extra), (0, 0)))

    sea = sea_mask.astype(F32)[:, None, :]
    spread = jnp.pad(spread, ((0, extra), (0, extra)))
    tile = (tile_rows, padded, lanes)
    f_tile = pltpu.VMEM(tile, F32)
    scratch = [
        pltpu.VMEM((n_blocks, count, *tile), BF16),
        pltpu.VMEM((n_blocks, *tile), BF16),
        pltpu.VMEM(tile, BF16),
    ]
    scratch += [f_tile] * 9
    scratch += [
        pltpu.VMEM((ITERATIONS, 2, lanes), F32),
        pltpu.VMEM((ITERATIONS, n_dev, 2, lanes), F32),
        pltpu.VMEM((grid_rows + 2, SUB, width), F32),
        pltpu.VMEM((grid_rows + 2, SUB, width), F32),
    ]
    for level in range(GRIDS):
        scratch += [pltpu.VMEM((grid_rows // 2**level + 2, SUB, width), F32)] * 3
    dma = pltpu.SemaphoreType.DMA
    scratch += [
        dma((n_blocks,)),
        dma((n_blocks,)),
        dma((groups,)),
        dma((n_dev,)),
        dma((n_dev,)),
        dma((groups,)),
        dma((ITERATIONS, n_dev)),
        dma((ITERATIONS, n_dev)),
        dma((n_blocks,)),
        dma((n_blocks,)),
    ]
    vmem = pl.BlockSpec(memory_space=pltpu.VMEM)
    increment, alpha_fields = pl.pallas_call(
        functools.partial(kernel, sizes, groups),
        out_shape=(
            jax.ShapeDtypeStruct(tile, F32),
            jax.ShapeDtypeStruct((count, n_blocks, *tile), BF16),
        ),
        in_specs=[vmem] * 6,
        out_specs=(vmem, vmem),
        scratch_shapes=scratch,
        compiler_params=pltpu.CompilerParams(
            collective_id=0, has_side_effects=True, vmem_limit_bytes=60 * 2**20
        ),
        name="window",
    )(by_row, spread, sea, field(innovations), field(obs_error), field(static_scale))
    increment = increment[:, :layers].transpose(1, 0, 2)
    alpha_fields = alpha_fields.reshape(count, rows, padded, lanes)[:, :, :layers]
    return increment, alpha_fields.transpose(0, 2, 1, 3)


def solution(mesh):
    in_specs = (
        P(("ens", "gx"), None, None, "gy"),
        P(),
        P(("ens", "gx"), "gy"),
        P(None, ("ens", "gx"), "gy"),
        P(None, ("ens", "gx"), "gy"),
        P(None, ("ens", "gx"), "gy"),
    )
    out_specs = (P(None, ("ens", "gx"), "gy"), P(("ens", "gx"), None, None, "gy"))
    sizes = tuple(mesh.shape[axis] for axis in ("ens", "gx", "gy"))
    return jax.shard_map(
        functools.partial(local, sizes),
        mesh=mesh,
        in_specs=in_specs,
        out_specs=out_specs,
        check_vma=False,
    )
```

```python
import functools

import jax
import jax.numpy as jnp
from jax import lax
from jax.experimental import pallas as pl
from jax.experimental.pallas import tpu as pltpu
from jax.sharding import PartitionSpec as P

GRIDS = 3
SWEEPS = 2
COARSE_SWEEPS = 4
ITERATIONS = 3
SUB = 8
LANES = 128

diffusivity = 16.0
damping = 0.8
MESH = pl.DeviceIdType.MESH
F32 = jnp.float32
BF16 = jnp.bfloat16


def strength_of(level):
    return diffusivity / 4.0**level


def lane_index(width):
    return lax.broadcasted_iota(jnp.int32, (SUB, width), 1)


def over_rows(count, body):
    chunk = min(SUB, count)

    @pl.loop(0, count // chunk)
    def _(block):
        start = block * chunk
        for row in range(chunk):
            body(start + row)


def neighbours(ref, row, step):
    here = ref[row + 1]
    width = here.shape[-1]
    lane = lane_index(width)
    left = jnp.where(lane < step, 0.0, pltpu.roll(here, step, 1))
    right = jnp.where(lane >= width - step, 0.0, pltpu.roll(here, width - step, 1))
    return here, ref[row] + ref[row + 2] + left + right


def relax(src, source, dst, rows, level, scale=None):
    strength = strength_of(level)
    factor = damping / (1.0 + 4.0 * strength)

    def body(row):
        here, around = neighbours(src, row, 2**level)
        if scale is not None:
            here, around = here * scale, around * scale
        dst[row + 1] = (1.0 - damping) * here + factor * (source[row + 1] + strength * around)

    over_rows(rows, body)


def restrict_remainder(src, source, dst, rows, level):
    strength = strength_of(level)
    step = 2**level

    def one(row):
        here, around = neighbours(src, row, step)
        left_over = source[row + 1] - (1.0 + 4.0 * strength) * here + strength * around
        return left_over

    def body(row):
        both = one(2 * row) + one(2 * row + 1)
        width = both.shape[-1]
        even = lax.rem(lane_index(width) // step, 2) == 0
        other = jnp.where(even, pltpu.roll(both, width - step, 1), pltpu.roll(both, step, 1))
        dst[row + 1] = 0.25 * (both + other)

    over_rows(rows // 2, body)


def add_prolonged(dst, coarse, rows):
    def body(row):
        extra = coarse[row + 1]
        dst[2 * row + 1] = dst[2 * row + 1] + extra
        dst[2 * row + 2] = dst[2 * row + 2] + extra

    over_rows(rows // 2, body)


def vcycle(levels, level, rows):
    source, first, second = levels[level]
    factor = damping / (1.0 + 4.0 * strength_of(level))
    if level == GRIDS - 1:
        relax(source, source, first, rows, level, factor)
        for _ in range(COARSE_SWEEPS - 2):
            relax(first, source, second, rows, level)
            first, second = second, first
        return first
    relax(source, source, first, rows, level, factor)
    for _ in range(SWEEPS - 2):
        relax(first, source, second, rows, level)
        first, second = second, first
    restrict_remainder(first, source, levels[level + 1][0], rows, level)
    coarse = vcycle(levels, level + 1, rows // 2)
    add_prolonged(first, coarse, rows)
    for _ in range(SWEEPS):
        relax(first, source, second, rows, level)
        first, second = second, first
    return first


def kernel(
    sizes,
    groups,
    members,
    spread,
    sea,
    innovations,
    obs_error,
    scale,
    increment,
    alpha_fields,
    gathered,
    r_send,
    s_recv,
    residual,
    along,
    cov_dir,
    cov_res,
    total,
    image,
    f_send,
    back,
    p_send,
    p_recv,
    f_along,
    *rest,
):
    n_ens, n_gx, n_gy = sizes
    level_refs = rest[: 3 * GRIDS]
    (f_ssem, f_rsem, b_ssem, b_rsem, p_ssem, p_rsem, r_ssem, r_rsem, s_ssem, s_rsem) = rest[3 * GRIDS :]
    levels = [level_refs[3 * g : 3 * g + 3] for g in range(GRIDS)]
    f_res, f_recv = levels[0][0], levels[0][2]
    n_blocks = n_ens * n_gx
    n_dev = n_blocks * n_gy
    spacing = n_dev // groups
    block = lax.axis_index("ens") * n_gx + lax.axis_index("gx")
    column = lax.axis_index("gy")
    me = block * n_gy + column
    is_owner = (lax.rem(me, spacing) == 0) & (me // spacing < groups)
    my_group = jnp.minimum(me // spacing, groups - 1)
    tile_rows = innovations.shape[0]
    layers = innovations.shape[1]
    count = members.shape[0]
    grid_rows = tile_rows * n_blocks

    def device(rank):
        return (rank // (n_gx * n_gy), lax.rem(rank // n_gy, n_gx), lax.rem(rank, n_gy))

    def group_rows(group):
        return pl.ds(pl.multiple_of(group * SUB, SUB), SUB)

    def grid_slot(ref, rank):
        rows = pl.ds((rank // n_gy) * tile_rows + 1, tile_rows)
        lanes = pl.ds(pl.multiple_of(lax.rem(rank, n_gy) * LANES, LANES), LANES)
        return ref.at[rows, :, lanes]

    def send(src, dst, send_sem, recv_sem, rank):
        @pl.when(rank == me)
        def _():
            pltpu.make_async_copy(src, dst, recv_sem).start()

        @pl.when(rank != me)
        def _():
            pltpu.make_async_remote_copy(
                src_ref=src,
                dst_ref=dst,
                send_sem=send_sem,
                recv_sem=recv_sem,
                device_id=device(rank),
                device_id_type=MESH,
            ).start()

    def sent(src, send_sem, rank):
        @pl.when(rank != me)
        def _():
            pltpu.make_async_copy(src, src, send_sem).wait()

    def arrived(dst, recv_sem):
        pltpu.make_async_copy(dst, dst, recv_sem).wait()

    barrier = pltpu.get_barrier_semaphore()

    @pl.loop(1, n_dev)
    def _(step):
        pl.semaphore_signal(
            barrier, inc=1, device_id=device(lax.rem(me + step, n_dev)), device_id_type=MESH
        )

    for r in range(tile_rows):
        start = innovations[r]
        residual[r] = start
        f_send[r] = jnp.zeros(f_send.shape[1:], F32)
        f_send[r, :layers] = scale[r] * (sea[r] * start)
        r_send[r] = (sea[r] * start).astype(BF16)
        zero = jnp.zeros_like(start)
        for ref in (along, cov_dir, increment):
            ref[r] = zero

    @pl.when(is_owner)
    def _():
        for source, first, second in levels:
            for ref in (source, first, second):
                edge = jnp.zeros(ref.shape[1:], F32)
                ref[0] = edge
                ref[ref.shape[0] - 1] = edge

        def clear(row):
            f_along[row + 1] = jnp.zeros(f_along.shape[1:], F32)
            f_res[row + 1] = jnp.zeros(f_res.shape[1:], F32)

        over_rows(grid_rows, clear)

    pl.semaphore_wait(barrier, n_dev - 1)

    def send_source():
        @pl.loop(0, groups)
        def _(group):
            send(
                f_send.at[:, group_rows(group), :],
                grid_slot(f_recv, me),
                f_ssem.at[group],
                f_rsem.at[me],
                group * spacing,
            )

    def source_sent():
        @pl.loop(0, groups)
        def _(group):
            sent(f_send.at[:, group_rows(group), :], f_ssem.at[group], group * spacing)

    def part_of(origin):
        return alpha_fields.at[0, pl.ds(origin * tile_rows, tile_rows)]

    def send_residual(iteration):
        @pl.loop(0, n_blocks)
        def _(step):
            target = lax.rem(block + step, n_blocks)
            send(
                r_send,
                gathered.at[iteration, block],
                r_ssem.at[target],
                r_rsem.at[iteration, block],
                target * n_gy + column,
            )

    def residual_sent():
        @pl.loop(0, n_blocks)
        def _(target):
            sent(r_send, r_ssem.at[target], target * n_gy + column)

    send_source()
    send_residual(0)

    def mix(values, vector):
        product = [
            (values[r].astype(F32) * vector[r]).astype(BF16) for r in range(tile_rows)
        ]
        mixed = jnp.dot(
            spread[...], jnp.concatenate(product, axis=1), preferred_element_type=F32
        )
        return [mixed[:, r * LANES : (r + 1) * LANES] for r in range(tile_rows)]

    def iterate(iteration, carry):
        alpha, ratio, norm, along_terms, weight_terms = carry

        @pl.when(is_owner)
        def _():
            @pl.loop(0, n_dev)
            def _(rank):
                arrived(grid_slot(f_recv, rank), f_rsem.at[rank])

            def advance(row):
                new = f_recv[row + 1] + ratio * f_along[row + 1]
                f_along[row + 1] = new
                f_res[row + 1] = f_res[row + 1] - alpha * new

            over_rows(grid_rows, advance)
            result = vcycle(levels, 0, grid_rows)

            @pl.loop(0, n_dev)
            def _(rank):
                send(
                    grid_slot(result, rank),
                    back.at[:, group_rows(my_group), :],
                    b_ssem.at[rank],
                    b_rsem.at[my_group],
                    rank,
                )

        @pl.loop(0, n_blocks)
        def _(step):
            origin = lax.rem(block - step + n_blocks, n_blocks)
            arrived(gathered.at[iteration, origin], r_rsem.at[iteration, origin])
            for r in range(tile_rows):
                image[r] = gathered[iteration, origin, r].astype(F32)
                total[r] = jnp.zeros_like(total[r])

            @pl.loop(0, count)
            def _(k):
                values = [members[k, origin * tile_rows + r] for r in range(tile_rows)]
                mixed = mix(values, image)
                for r in range(tile_rows):
                    total[r] = total[r] + values[r].astype(F32) * mixed[r]

            @pl.when(step == 0)
            def _():
                for r in range(tile_rows):
                    cov_res[r] = total[r]

            @pl.when(step > 0)
            def _():
                for r in range(tile_rows):
                    alpha_fields[0, origin * tile_rows + r] = total[r].astype(BF16)
                send(
                    part_of(origin),
                    s_recv.at[block],
                    s_ssem.at[origin],
                    s_rsem.at[block],
                    origin * n_gy + column,
                )

        @pl.loop(1, n_blocks)
        def _(step):
            origin = lax.rem(block - step + n_blocks, n_blocks)
            arrived(s_recv.at[origin], s_rsem.at[origin])
            for r in range(tile_rows):
                cov_res[r] = cov_res[r] + s_recv[origin, r].astype(F32)

        @pl.loop(0, groups)
        def _(group):
            arrived(back.at[:, group_rows(group), :], b_rsem.at[group])

        source_sent()
        own = jnp.zeros((1, LANES), F32)
        cross = jnp.zeros((1, LANES), F32)
        for r in range(tile_rows):
            cov = sea[r] * (cov_res[r] + scale[r] * back[r, :layers])
            now = residual[r]
            img = cov + obs_error[r] * now
            cov_res[r] = cov
            image[r] = img
            f_send[r, :layers] = scale[r] * (sea[r] * img)
            own = own + jnp.sum(now * now, axis=0, keepdims=True)
            cross = cross + jnp.sum(now * img, axis=0, keepdims=True)
        p_send[iteration, 0:1] = own
        p_send[iteration, 1:2] = cross

        @pl.loop(0, n_dev)
        def _(step):
            rank = lax.rem(me + step, n_dev)
            send(
                p_send.at[iteration],
                p_recv.at[iteration, me],
                p_ssem.at[iteration, rank],
                p_rsem.at[iteration, me],
                rank,
            )

        @pl.when(iteration < ITERATIONS - 1)
        def _():
            send_source()

        @pl.loop(0, n_dev)
        def _(rank):
            arrived(p_recv.at[iteration, rank], p_rsem.at[iteration, rank])

        sums = jnp.sum(jnp.sum(p_recv[iteration], axis=0), axis=1, keepdims=True)
        norm_next, product = sums[0:1], sums[1:2]
        ratio = jnp.where(iteration == 0, 0.0, norm_next / norm)
        alpha = norm_next / (product - ratio * norm_next / alpha)
        along_terms = [
            ratio * term + jnp.where(iteration == n, 1.0, 0.0)
            for n, term in enumerate(along_terms)
        ]
        weight_terms = [w + alpha * d for w, d in zip(weight_terms, along_terms)]
        residual_sent()
        for r in range(tile_rows):
            img = image[r] + ratio * along[r]
            along[r] = img
            now = residual[r] - alpha * img
            residual[r] = now
            r_send[r] = (sea[r] * now).astype(BF16)

        @pl.when(iteration < ITERATIONS - 1)
        def _():
            send_residual(iteration + 1)

        for r in range(tile_rows):
            cov = cov_res[r] + ratio * cov_dir[r]
            cov_dir[r] = cov
            increment[r] = increment[r] + alpha * cov

        @pl.loop(1, n_blocks)
        def _(step):
            origin = lax.rem(block - step + n_blocks, n_blocks)
            sent(part_of(origin), s_ssem.at[origin], origin * n_gy + column)

        @pl.loop(0, n_dev)
        def _(rank):
            sent(p_send.at[iteration], p_ssem.at[iteration, rank], rank)

        @pl.when(is_owner)
        def _():
            @pl.loop(0, n_dev)
            def _(rank):
                sent(grid_slot(levels[0][1], rank), b_ssem.at[rank], rank)

        return alpha, ratio, norm_next, along_terms, weight_terms

    one = jnp.ones((1, 1), F32)
    none = [one * 0.0] * ITERATIONS
    state = lax.fori_loop(0, ITERATIONS, iterate, (-one, one * 0.0, one, none, none))
    weight_terms = state[-1]

    @pl.loop(0, n_blocks)
    def _(origin):
        for r in range(tile_rows):
            image[r] = sum(
                term * gathered[n, origin, r].astype(F32) for n, term in enumerate(weight_terms)
            )

        @pl.loop(0, count)
        def _(k):
            mixed = mix([members[k, origin * tile_rows + r] for r in range(tile_rows)], image)
            for r in range(tile_rows):
                alpha_fields[k, origin * tile_rows + r] = mixed[r].astype(BF16)


def local(sizes, members, spread, sea_mask, innovations, obs_error, static_scale):
    n_ens, n_gx, n_gy = sizes
    n_blocks = n_ens * n_gx
    n_dev = n_blocks * n_gy
    count, layers, rows, lanes = members.shape
    tile_rows = innovations.shape[1]
    groups = -(-layers // SUB)
    padded = groups * SUB
    grid_rows = rows
    width = lanes * n_gy

    def field(values):
        return values.transpose(1, 0, 2)

    sea = sea_mask.astype(F32)[:, None, :]
    tile = (tile_rows, layers, lanes)
    wide = (tile_rows, padded, lanes)
    f_tile = pltpu.VMEM(tile, F32)
    scratch = [
        pltpu.VMEM((ITERATIONS, n_blocks, *tile), BF16),
        pltpu.VMEM(tile, BF16),
        pltpu.VMEM((n_blocks, *tile), BF16),
    ]
    scratch += [f_tile] * 6
    scratch += [
        pltpu.VMEM(wide, F32),
        pltpu.VMEM(wide, F32),
        pltpu.VMEM((ITERATIONS, 2, lanes), F32),
        pltpu.VMEM((ITERATIONS, n_dev, 2, lanes), F32),
        pltpu.VMEM((grid_rows + 2, SUB, width), F32),
    ]
    for level in range(GRIDS):
        scratch += [pltpu.VMEM((grid_rows // 2**level + 2, SUB, width), F32)] * 3
    dma = pltpu.SemaphoreType.DMA
    scratch += [
        dma((groups,)),
        dma((n_dev,)),
        dma((n_dev,)),
        dma((groups,)),
        dma((ITERATIONS, n_dev)),
        dma((ITERATIONS, n_dev)),
        dma((n_blocks,)),
        dma((ITERATIONS, n_blocks)),
        dma((n_blocks,)),
        dma((n_blocks,)),
    ]
    vmem = pl.BlockSpec(memory_space=pltpu.VMEM)
    increment, alpha_fields = pl.pallas_call(
        functools.partial(kernel, sizes, groups),
        out_shape=(
            jax.ShapeDtypeStruct(tile, F32),
            jax.ShapeDtypeStruct((count, rows, layers, lanes), BF16),
        ),
        in_specs=[vmem] * 6,
        out_specs=(vmem, vmem),
        scratch_shapes=scratch,
        compiler_params=pltpu.CompilerParams(
            collective_id=0, has_side_effects=True, vmem_limit_bytes=64000 * 2**10
        ),
        name="window",
    )(members.transpose(0, 2, 1, 3), spread, sea, field(innovations), field(obs_error), field(static_scale))
    return increment.transpose(1, 0, 2), alpha_fields.transpose(0, 2, 1, 3)


def solution(mesh):
    in_specs = (
        P(("ens", "gx"), None, None, "gy"),
        P(),
        P(("ens", "gx"), "gy"),
        P(None, ("ens", "gx"), "gy"),
        P(None, ("ens", "gx"), "gy"),
        P(None, ("ens", "gx"), "gy"),
    )
    out_specs = (P(None, ("ens", "gx"), "gy"), P(("ens", "gx"), None, None, "gy"))
    sizes = tuple(mesh.shape[axis] for axis in ("ens", "gx", "gy"))
    return jax.shard_map(
        functools.partial(local, sizes),
        mesh=mesh,
        in_specs=in_specs,
        out_specs=out_specs,
        check_vma=False,
    )
```

```python
import functools

import jax
import jax.numpy as jnp
from jax import lax
from jax.experimental import pallas as pl
from jax.experimental.pallas import tpu as pltpu
from jax.sharding import PartitionSpec as P

GRIDS = 3
SWEEPS = 2
COARSE_SWEEPS = 4
ITERATIONS = 3
SUB = 8
LANES = 128

diffusivity = 16.0
damping = 0.8
MESH = pl.DeviceIdType.MESH
F32 = jnp.float32
BF16 = jnp.bfloat16


def strength_of(level):
    return diffusivity / 4.0**level


def lane_index(width):
    return lax.broadcasted_iota(jnp.int32, (SUB, width), 1)


def over_rows(count, body):
    chunk = min(SUB, count)

    @pl.loop(0, count // chunk)
    def _(block):
        start = block * chunk
        for row in range(chunk):
            body(start + row)


def neighbours(ref, row, step):
    here = ref[row + 1]
    width = here.shape[-1]
    lane = lane_index(width)
    left = jnp.where(lane < step, 0.0, pltpu.roll(here, step, 1))
    right = jnp.where(lane >= width - step, 0.0, pltpu.roll(here, width - step, 1))
    return here, ref[row] + ref[row + 2] + left + right


def relax(src, source, dst, rows, level, scale=None):
    strength = strength_of(level)
    factor = damping / (1.0 + 4.0 * strength)

    def body(row):
        here, around = neighbours(src, row, 2**level)
        if scale is not None:
            here, around = here * scale, around * scale
        dst[row + 1] = (1.0 - damping) * here + factor * (source[row + 1] + strength * around)

    over_rows(rows, body)


def restrict_remainder(src, source, dst, rows, level):
    strength = strength_of(level)
    step = 2**level

    def one(row):
        here, around = neighbours(src, row, step)
        left_over = source[row + 1] - (1.0 + 4.0 * strength) * here + strength * around
        return left_over

    def body(row):
        both = one(2 * row) + one(2 * row + 1)
        width = both.shape[-1]
        even = lax.rem(lane_index(width) // step, 2) == 0
        other = jnp.where(even, pltpu.roll(both, width - step, 1), pltpu.roll(both, step, 1))
        dst[row + 1] = 0.25 * (both + other)

    over_rows(rows // 2, body)


def add_prolonged(dst, coarse, rows):
    def body(row):
        extra = coarse[row + 1]
        dst[2 * row + 1] = dst[2 * row + 1] + extra
        dst[2 * row + 2] = dst[2 * row + 2] + extra

    over_rows(rows // 2, body)


def vcycle(levels, level, rows):
    source, first, second = levels[level]
    factor = damping / (1.0 + 4.0 * strength_of(level))
    if level == GRIDS - 1:
        relax(source, source, first, rows, level, factor)
        for _ in range(COARSE_SWEEPS - 2):
            relax(first, source, second, rows, level)
            first, second = second, first
        return first
    relax(source, source, first, rows, level, factor)
    for _ in range(SWEEPS - 2):
        relax(first, source, second, rows, level)
        first, second = second, first
    restrict_remainder(first, source, levels[level + 1][0], rows, level)
    coarse = vcycle(levels, level + 1, rows // 2)
    add_prolonged(first, coarse, rows)
    for _ in range(SWEEPS):
        relax(first, source, second, rows, level)
        first, second = second, first
    return first


def kernel(
    sizes,
    groups,
    members,
    spread,
    sea,
    innovations,
    obs_error,
    scale,
    increment,
    alpha_fields,
    gathered,
    r_send,
    s_recv,
    e_recv,
    own_sum,
    residual,
    along,
    cov_dir,
    cov_res,
    total,
    image,
    f_send,
    back,
    p_send,
    p_recv,
    f_along,
    *rest,
):
    n_ens, n_gx, n_gy = sizes
    level_refs = rest[: 3 * GRIDS]
    (f_ssem, f_rsem, b_ssem, b_rsem, p_ssem, p_rsem, r_ssem, r_rsem, x_ssem, s_ssem, s_rsem, e_ssem, e_rsem) = rest[3 * GRIDS :]
    levels = [level_refs[3 * g : 3 * g + 3] for g in range(GRIDS)]
    f_res, f_recv = levels[0][0], levels[0][2]
    n_blocks = n_ens * n_gx
    n_dev = n_blocks * n_gy
    spacing = n_dev // groups
    my_ens = lax.axis_index("ens")
    my_gx = lax.axis_index("gx")
    block = my_ens * n_gx + my_gx
    column = lax.axis_index("gy")
    me = block * n_gy + column
    is_owner = (lax.rem(me, spacing) == 0) & (me // spacing < groups)
    my_group = jnp.minimum(me // spacing, groups - 1)
    tile_rows = innovations.shape[0]
    layers = innovations.shape[1]
    count = members.shape[0]
    grid_rows = tile_rows * n_blocks

    def device(rank):
        return (rank // (n_gx * n_gy), lax.rem(rank // n_gy, n_gx), lax.rem(rank, n_gy))

    def group_rows(group):
        return pl.ds(pl.multiple_of(group * SUB, SUB), SUB)

    def grid_slot(ref, rank):
        rows = pl.ds((rank // n_gy) * tile_rows + 1, tile_rows)
        lanes = pl.ds(pl.multiple_of(lax.rem(rank, n_gy) * LANES, LANES), LANES)
        return ref.at[rows, :, lanes]

    def send(src, dst, send_sem, recv_sem, rank):
        @pl.when(rank == me)
        def _():
            pltpu.make_async_copy(src, dst, recv_sem).start()

        @pl.when(rank != me)
        def _():
            pltpu.make_async_remote_copy(
                src_ref=src,
                dst_ref=dst,
                send_sem=send_sem,
                recv_sem=recv_sem,
                device_id=device(rank),
                device_id_type=MESH,
            ).start()

    def sent(src, send_sem, rank):
        @pl.when(rank != me)
        def _():
            pltpu.make_async_copy(src, src, send_sem).wait()

    def arrived(dst, recv_sem):
        pltpu.make_async_copy(dst, dst, recv_sem).wait()

    barrier = pltpu.get_barrier_semaphore()

    @pl.loop(1, n_dev)
    def _(step):
        pl.semaphore_signal(
            barrier, inc=1, device_id=device(lax.rem(me + step, n_dev)), device_id_type=MESH
        )

    for r in range(tile_rows):
        start = innovations[r]
        residual[r] = start
        f_send[r] = jnp.zeros(f_send.shape[1:], F32)
        f_send[r, :layers] = scale[r] * (sea[r] * start)
        r_send[r] = (sea[r] * start).astype(BF16)
        zero = jnp.zeros_like(start)
        for ref in (along, cov_dir, increment):
            ref[r] = zero

    @pl.when(is_owner)
    def _():
        for source, first, second in levels:
            for ref in (source, first, second):
                edge = jnp.zeros(ref.shape[1:], F32)
                ref[0] = edge
                ref[ref.shape[0] - 1] = edge

        def clear(row):
            f_along[row + 1] = jnp.zeros(f_along.shape[1:], F32)
            f_res[row + 1] = jnp.zeros(f_res.shape[1:], F32)

        over_rows(grid_rows, clear)

    pl.semaphore_wait(barrier, n_dev - 1)

    def send_source():
        @pl.loop(0, groups)
        def _(group):
            send(
                f_send.at[:, group_rows(group), :],
                grid_slot(f_recv, me),
                f_ssem.at[group],
                f_rsem.at[me],
                group * spacing,
            )

    def source_sent():
        @pl.loop(0, groups)
        def _(group):
            sent(f_send.at[:, group_rows(group), :], f_ssem.at[group], group * spacing)

    def part_of(origin):
        return alpha_fields.at[0, pl.ds(origin * tile_rows, tile_rows)]

    def peer(ens, gx):
        return (ens * n_gx + gx) * n_gy + column

    def send_residual(iteration):
        def to(ens):
            send(
                r_send,
                gathered.at[iteration, block],
                r_ssem.at[ens],
                r_rsem.at[iteration, block],
                peer(ens, my_gx),
            )

        @pl.loop(0, n_ens)
        def _(step):
            to(lax.rem(my_ens + step, n_ens))

    def residual_sent():
        @pl.loop(0, n_ens)
        def _(ens):
            sent(r_send, r_ssem.at[ens], peer(ens, my_gx))

    send_source()
    send_residual(0)

    def mix(values, vector):
        product = [
            (values[r].astype(F32) * vector[r]).astype(BF16) for r in range(tile_rows)
        ]
        mixed = jnp.dot(
            spread[...], jnp.concatenate(product, axis=1), preferred_element_type=F32
        )
        return [mixed[:, r * LANES : (r + 1) * LANES] for r in range(tile_rows)]

    def iterate(iteration, carry):
        alpha, ratio, norm, along_terms, weight_terms = carry

        @pl.when(is_owner)
        def _():
            @pl.loop(0, n_dev)
            def _(rank):
                arrived(grid_slot(f_recv, rank), f_rsem.at[rank])

            def advance(row):
                new = f_recv[row + 1] + ratio * f_along[row + 1]
                f_along[row + 1] = new
                f_res[row + 1] = f_res[row + 1] - alpha * new

            over_rows(grid_rows, advance)
            result = vcycle(levels, 0, grid_rows)

            @pl.loop(0, n_dev)
            def _(rank):
                send(
                    grid_slot(result, rank),
                    back.at[:, group_rows(my_group), :],
                    b_ssem.at[rank],
                    b_rsem.at[my_group],
                    rank,
                )

        def tile_of(origin):
            return gathered.at[iteration, origin]

        @pl.loop(0, n_ens)
        def _(step):
            origin = lax.rem(my_ens - step + n_ens, n_ens) * n_gx + my_gx
            arrived(tile_of(origin), r_rsem.at[iteration, origin])

            @pl.loop(1, n_gx)
            def _(hop):
                gx = lax.rem(my_gx + hop, n_gx)
                send(
                    tile_of(origin),
                    tile_of(origin),
                    x_ssem.at[origin // n_gx, gx],
                    r_rsem.at[iteration, origin],
                    peer(my_ens, gx),
                )

        def partial_sum(origin):
            for r in range(tile_rows):
                image[r] = gathered[iteration, origin, r].astype(F32)
                total[r] = jnp.zeros_like(total[r])

            @pl.loop(0, count)
            def _(k):
                values = [members[k, origin * tile_rows + r] for r in range(tile_rows)]
                mixed = mix(values, image)
                for r in range(tile_rows):
                    total[r] = total[r] + values[r].astype(F32) * mixed[r]

        @pl.loop(0, n_ens)
        def _(ens):
            partial_sum(ens * n_gx + my_gx)
            for r in range(tile_rows):
                own_sum[ens, r] = total[r]

        @pl.loop(1, n_gx)
        def _(hop):
            gx = lax.rem(my_gx + hop, n_gx)

            @pl.loop(1, n_ens + 1)
            def _(step):
                ens = lax.rem(my_ens - step + n_ens, n_ens)
                origin = ens * n_gx + gx
                arrived(tile_of(origin), r_rsem.at[iteration, origin])
                partial_sum(origin)
                for r in range(tile_rows):
                    alpha_fields[0, origin * tile_rows + r] = total[r].astype(BF16)
                send(
                    part_of(origin),
                    s_recv.at[my_gx, ens],
                    s_ssem.at[ens, gx],
                    s_rsem.at[my_gx, ens],
                    peer(my_ens, gx),
                )

        @pl.loop(1, n_ens + 1)
        def _(step):
            ens = lax.rem(my_ens - step + n_ens, n_ens)
            origin = ens * n_gx + my_gx

            @pl.loop(1, n_gx)
            def _(hop):
                gx = lax.rem(my_gx + hop, n_gx)
                arrived(s_recv.at[gx, ens], s_rsem.at[gx, ens])
                for r in range(tile_rows):
                    own_sum[ens, r] = own_sum[ens, r] + s_recv[gx, ens, r].astype(F32)

            @pl.when(step < n_ens)
            def _():
                for r in range(tile_rows):
                    alpha_fields[0, origin * tile_rows + r] = own_sum[ens, r].astype(BF16)
                send(
                    part_of(origin),
                    e_recv.at[my_ens],
                    e_ssem.at[ens],
                    e_rsem.at[my_ens],
                    peer(ens, my_gx),
                )

        for r in range(tile_rows):
            cov_res[r] = own_sum[my_ens, r]

        @pl.loop(1, n_ens)
        def _(step):
            ens = lax.rem(my_ens - step + n_ens, n_ens)
            arrived(e_recv.at[ens], e_rsem.at[ens])
            for r in range(tile_rows):
                cov_res[r] = cov_res[r] + e_recv[ens, r].astype(F32)

        @pl.loop(0, groups)
        def _(group):
            arrived(back.at[:, group_rows(group), :], b_rsem.at[group])

        source_sent()
        own = jnp.zeros((1, LANES), F32)
        cross = jnp.zeros((1, LANES), F32)
        for r in range(tile_rows):
            cov = sea[r] * (cov_res[r] + scale[r] * back[r, :layers])
            now = residual[r]
            img = cov + obs_error[r] * now
            cov_res[r] = cov
            image[r] = img
            f_send[r, :layers] = scale[r] * (sea[r] * img)
            own = own + jnp.sum(now * now, axis=0, keepdims=True)
            cross = cross + jnp.sum(now * img, axis=0, keepdims=True)
        p_send[iteration, 0:1] = own
        p_send[iteration, 1:2] = cross

        @pl.loop(0, n_dev)
        def _(step):
            rank = lax.rem(me + step, n_dev)
            send(
                p_send.at[iteration],
                p_recv.at[iteration, me],
                p_ssem.at[iteration, rank],
                p_rsem.at[iteration, me],
                rank,
            )

        @pl.when(iteration < ITERATIONS - 1)
        def _():
            send_source()

        @pl.loop(0, n_dev)
        def _(rank):
            arrived(p_recv.at[iteration, rank], p_rsem.at[iteration, rank])

        sums = jnp.sum(jnp.sum(p_recv[iteration], axis=0), axis=1, keepdims=True)
        norm_next, product = sums[0:1], sums[1:2]
        ratio = jnp.where(iteration == 0, 0.0, norm_next / norm)
        alpha = norm_next / (product - ratio * norm_next / alpha)
        along_terms = [
            ratio * term + jnp.where(iteration == n, 1.0, 0.0)
            for n, term in enumerate(along_terms)
        ]
        weight_terms = [w + alpha * d for w, d in zip(weight_terms, along_terms)]
        residual_sent()
        for r in range(tile_rows):
            img = image[r] + ratio * along[r]
            along[r] = img
            now = residual[r] - alpha * img
            residual[r] = now
            r_send[r] = (sea[r] * now).astype(BF16)

        @pl.when(iteration < ITERATIONS - 1)
        def _():
            send_residual(iteration + 1)

        for r in range(tile_rows):
            cov = cov_res[r] + ratio * cov_dir[r]
            cov_dir[r] = cov
            increment[r] = increment[r] + alpha * cov

        @pl.loop(0, n_ens)
        def _(ens):
            @pl.loop(1, n_gx)
            def _(hop):
                gx = lax.rem(my_gx + hop, n_gx)
                sent(part_of(block), s_ssem.at[ens, gx], peer(my_ens, gx))
                sent(tile_of(block), x_ssem.at[ens, gx], peer(my_ens, gx))

            sent(part_of(block), e_ssem.at[ens], peer(ens, my_gx))

        @pl.loop(0, n_dev)
        def _(rank):
            sent(p_send.at[iteration], p_ssem.at[iteration, rank], rank)

        @pl.when(is_owner)
        def _():
            @pl.loop(0, n_dev)
            def _(rank):
                sent(grid_slot(levels[0][1], rank), b_ssem.at[rank], rank)

        return alpha, ratio, norm_next, along_terms, weight_terms

    one = jnp.ones((1, 1), F32)
    none = [one * 0.0] * ITERATIONS
    state = lax.fori_loop(0, ITERATIONS, iterate, (-one, one * 0.0, one, none, none))
    weight_terms = state[-1]

    @pl.loop(0, n_blocks)
    def _(origin):
        for r in range(tile_rows):
            image[r] = sum(
                term * gathered[n, origin, r].astype(F32) for n, term in enumerate(weight_terms)
            )

        @pl.loop(0, count)
        def _(k):
            mixed = mix([members[k, origin * tile_rows + r] for r in range(tile_rows)], image)
            for r in range(tile_rows):
                alpha_fields[k, origin * tile_rows + r] = mixed[r].astype(BF16)


def local(sizes, members, spread, sea_mask, innovations, obs_error, static_scale):
    n_ens, n_gx, n_gy = sizes
    n_blocks = n_ens * n_gx
    n_dev = n_blocks * n_gy
    count, layers, rows, lanes = members.shape
    tile_rows = innovations.shape[1]
    groups = -(-layers // SUB)
    padded = groups * SUB
    grid_rows = rows
    width = lanes * n_gy

    def field(values):
        return values.transpose(1, 0, 2)

    sea = sea_mask.astype(F32)[:, None, :]
    tile = (tile_rows, layers, lanes)
    wide = (tile_rows, padded, lanes)
    f_tile = pltpu.VMEM(tile, F32)
    scratch = [
        pltpu.VMEM((ITERATIONS, n_blocks, *tile), BF16),
        pltpu.VMEM(tile, BF16),
        pltpu.VMEM((n_gx, n_ens, *tile), BF16),
        pltpu.VMEM((n_ens, *tile), BF16),
        pltpu.VMEM((n_ens, *tile), F32),
    ]
    scratch += [f_tile] * 6
    scratch += [
        pltpu.VMEM(wide, F32),
        pltpu.VMEM(wide, F32),
        pltpu.VMEM((ITERATIONS, 2, lanes), F32),
        pltpu.VMEM((ITERATIONS, n_dev, 2, lanes), F32),
        pltpu.VMEM((grid_rows + 2, SUB, width), F32),
    ]
    for level in range(GRIDS):
        scratch += [pltpu.VMEM((grid_rows // 2**level + 2, SUB, width), F32)] * 3
    dma = pltpu.SemaphoreType.DMA
    scratch += [
        dma((groups,)),
        dma((n_dev,)),
        dma((n_dev,)),
        dma((groups,)),
        dma((ITERATIONS, n_dev)),
        dma((ITERATIONS, n_dev)),
        dma((n_ens,)),
        dma((ITERATIONS, n_blocks)),
        dma((n_ens, n_gx)),
        dma((n_ens, n_gx)),
        dma((n_gx, n_ens)),
        dma((n_ens,)),
        dma((n_ens,)),
    ]
    vmem = pl.BlockSpec(memory_space=pltpu.VMEM)
    increment, alpha_fields = pl.pallas_call(
        functools.partial(kernel, sizes, groups),
        out_shape=(
            jax.ShapeDtypeStruct(tile, F32),
            jax.ShapeDtypeStruct((count, rows, layers, lanes), BF16),
        ),
        in_specs=[vmem] * 6,
        out_specs=(vmem, vmem),
        scratch_shapes=scratch,
        compiler_params=pltpu.CompilerParams(
            collective_id=0, has_side_effects=True, vmem_limit_bytes=64000 * 2**10
        ),
        name="window",
    )(members.transpose(0, 2, 1, 3), spread, sea, field(innovations), field(obs_error), field(static_scale))
    return increment.transpose(1, 0, 2), alpha_fields.transpose(0, 2, 1, 3)


def solution(mesh):
    in_specs = (
        P(("ens", "gx"), None, None, "gy"),
        P(),
        P(("ens", "gx"), "gy"),
        P(None, ("ens", "gx"), "gy"),
        P(None, ("ens", "gx"), "gy"),
        P(None, ("ens", "gx"), "gy"),
    )
    out_specs = (P(None, ("ens", "gx"), "gy"), P(("ens", "gx"), None, None, "gy"))
    sizes = tuple(mesh.shape[axis] for axis in ("ens", "gx", "gy"))
    return jax.shard_map(
        functools.partial(local, sizes),
        mesh=mesh,
        in_specs=in_specs,
        out_specs=out_specs,
        check_vma=False,
    )
```
